32 devices in a mesh: parts: 2 (over x), wide: 16 (over z, y, core).
Axes of the slice: x: 2, y: 2, z: 4, core: 2. Of those that a mesh axis runs over, the one named last changes fastest.
Arguments:
- tokens: bfloat16 [384, 7168], P(('parts', 'wide')), parts along dimension 0, may hold values from -6 to 6
- expert_ids: int32 [384, 8], P(('parts', 'wide')), parts along dimension 0, may hold values from 0 to 15, as said below
- gates: float32 [384, 8], P(('parts', 'wide')), parts along dimension 0, may hold values from 0.1 to 1
- w_gate: bfloat16 [2, 7168, 8192], P(None, None, 'wide'), may hold values from -0.0625 to 0.0625
- w_up: bfloat16 [2, 7168, 8192], P(None, None, 'wide'), may hold values from -0.0625 to 0.0625
- w_down: bfloat16 [2, 8192, 7168], P(None, 'wide'), may hold values from -0.1875 to 0.1875
Outputs:
- moe_out: bfloat16 [384, 7168], P(('parts', 'wide')), parts along dimension 0
The draws below stay inside these ranges and needn't reach their ends.
There are 2 independent parts, one for each index of `parts`. The reference program is written for one: setup_inputs(seed, part) draws one part's arguments, and reference() takes and returns one part's arrays. A program takes and returns all parts, laid end to end along the dimension named above; an argument that names none is the same for every part. Nothing has to cross between parts.
Inputs may be any that keep to these rules, and one draw needn't show every extreme that they name: `expert_ids`: each row names the 2 experts g * 2 to g * 2 + 1 of each of 4 different groups g, in any order; in each part one group is named by every row.
All inputs are finite; a program needn't handle non-finite values.
Results may differ from the reference program's by a relative error of at most 0.0064.
Values may be sent and summed in bfloat16 or wider, within the bound.
A program may use at most 128 MiB of HBM per device.

```python
import jax
import jax.numpy as jnp
from jax import lax

D = 7168
GROUPS = 8
TOPG = 4
TOPK = 8
EXP_G = 2
FH = 1024
TOKENS = 192
EXPERTS = 16
N_WIDE = 16


def draw_expert_ids(key, part):
    key_hot, key_group, key_order = jax.random.split(jax.random.fold_in(key, 7103), 3)
    hot_group = jax.random.randint(key_hot, (), 0, GROUPS)
    group_range = jnp.arange(GROUPS, dtype=jnp.int32)
    noise = jax.random.randint(key_group, (TOKENS, GROUPS), 0, 1 << 20)
    scores = noise * GROUPS + group_range[None, :]
    scores = jnp.where(group_range[None, :] == hot_group, -1, scores)
    chosen_groups = jnp.argsort(scores, axis=1, stable=True)[:, :TOPG]
    experts_named = (chosen_groups[:, :, None] * EXP_G + jnp.arange(EXP_G, dtype=jnp.int32)[None, None, :]).reshape(TOKENS, TOPK)
    order_noise = jax.random.randint(key_order, (TOKENS, TOPK), 0, 1 << 20) * TOPK + jnp.arange(TOPK, dtype=jnp.int32)[None, :]
    shuffle = jnp.argsort(order_noise, axis=1, stable=True)
    return jnp.take_along_axis(experts_named, shuffle, axis=1).astype(jnp.int32)


def block_scale(stream_key, dims, cuts, least, top_value):
    factor_of, own = 1.0, jax.random.fold_in(stream_key, 6)
    for axis_at, parts in cuts:
        heights = jnp.exp(jax.random.uniform(jax.random.fold_in(own, axis_at), (parts,), jnp.float32, least / len(cuts), top_value / len(cuts)))
        factor_of = factor_of * jnp.repeat(heights, dims[axis_at] // parts).reshape([-1 if axis == axis_at else 1 for axis in range(len(dims))])
    return factor_of


def centred(key, shape, spread, limit, pieces=(), kind=jnp.bfloat16):
    result = jax.random.normal(key, shape, jnp.float32) * spread
    if len(pieces) > 0:
        result = block_scale(key, shape, pieces, -0.22, 0.18) * result
    return jnp.clip(result, min=-limit, max=limit).astype(kind)


def setup_inputs(seed: int = 0, part: int = 0) -> dict:
    keys = jax.random.split(jax.random.key(seed), 7)
    part_keys = jax.random.split(jax.random.fold_in(keys[6], part), 7)
    return {
        "tokens": centred(part_keys[0], (TOKENS, D), 1.0, 6.0, ((0, 16),)),
        "expert_ids": draw_expert_ids(jax.random.fold_in(jax.random.fold_in(keys[6], part), 71), part),
        "gates": jnp.clip(0.1 + 0.9 * jax.random.uniform(part_keys[2], (TOKENS, TOPK), jnp.float32) ** block_scale(part_keys[2], (TOKENS, TOPK), ((0, 16),), -0.2, 0.2), 0.1, 1.0),
        "w_gate": centred(keys[3], (EXP_G, D, GROUPS * FH), D ** -0.5, 0.0625, ((2, 16),)),
        "w_up": centred(keys[4], (EXP_G, D, GROUPS * FH), D ** -0.5, 0.0625, ((2, 16),)),
        "w_down": centred(keys[5], (EXP_G, GROUPS * FH, D), FH ** -0.5, 0.1875, ((1, 16),)),
    }


def reference(tokens, expert_ids, gates, w_gate, w_up, w_down):
    group_size = N_WIDE // GROUPS
    block_width = FH // group_size
    catalog = jnp.arange(EXPERTS, dtype=jnp.int32)
    picked = expert_ids[:, :, None] == catalog[None, None, :]
    route_weight = jnp.sum(jnp.where(picked, gates[:, :, None], jnp.float32(0.0)), axis=1).astype(jnp.bfloat16)

    def add_block(device, summed):
        device = jnp.asarray(device).astype(jnp.int32)
        group_index = device // group_size
        column_start = (device * block_width).astype(jnp.int32)
        gate_block = lax.dynamic_slice_in_dim(w_gate, column_start, block_width, 2)
        up_block = lax.dynamic_slice_in_dim(w_up, column_start, block_width, 2)
        down_block = lax.dynamic_slice_in_dim(w_down, column_start, block_width, 1)
        scales = lax.dynamic_slice_in_dim(route_weight, (group_index * EXP_G).astype(jnp.int32), EXP_G, 1).astype(jnp.float32)
        partial_value = jnp.zeros((TOKENS, D), jnp.float32)
        for expert in range(EXP_G):
            gate_value = jnp.dot(tokens, gate_block[expert], preferred_element_type=jnp.float32)
            lifted = jnp.dot(tokens, up_block[expert], preferred_element_type=jnp.float32)
            hidden = (jax.nn.silu(gate_value) * lifted).astype(jnp.bfloat16)
            partial_value = partial_value + scales[:, expert:expert + 1] * jnp.dot(hidden, down_block[expert], preferred_element_type=jnp.float32)
        rounded = lax.optimization_barrier(partial_value.astype(jnp.bfloat16))
        return summed + rounded.astype(jnp.float32)

    summed = lax.fori_loop(0, N_WIDE, add_block, jnp.zeros((TOKENS, D), jnp.float32))
    return summed.astype(jnp.bfloat16)
```

```python
import functools
import math

import jax
import jax.numpy as jnp
from jax import lax
from jax.experimental import pallas as pl
from jax.experimental.pallas import tpu as pltpu
from jax.sharding import PartitionSpec as P

GROUPS = 8
EXP_G = 2
CORES = 2
SIDES = 2
CHUNK = 256
LANES = 128
F32 = jnp.float32
BF16 = jnp.bfloat16


def floor_div(value, by):
    return jnp.floor((value + 0.5) * (1.0 / by))


def iota_f32(shape, dim):
    return lax.broadcasted_iota(jnp.int32, shape, dim).astype(F32)


def kernel(
    wide, rows, fold,
    x_ref, r_ref, wg_ref, wu_ref, wd_ref, out_ref,
    xb, rb, wgb, wub, wdb, acc, hid, perm, perm_back, packed, got_core, sum_side, got_side, sum_z, got_z, out_buf,
    w_sem, d_sem, own_sem, az_s, az_r, ay_s, ay_r, ac_s, ac_r, bz_s, bz_r, by_s, by_r, bc_s, bc_r, out_sem,
):
    zs = wide // (CORES * SIDES)
    chunks = x_ref.shape[0]
    hidden = wg_ref.shape[2]
    width = chunks * CHUNK
    unit = rows * fold
    units = wide
    groups = units // fold
    band = fold * rows
    pad_rows = r_ref.shape[0]

    me = lax.axis_index("wide")
    core = lax.rem(me, CORES)
    chip = me // CORES
    side = lax.rem(chip, SIDES)
    z = chip // SIDES
    other_core = 1 - core
    other_side = 1 - side

    def at(z_at, side_at, core_at):
        return {"wide": (z_at * SIDES + side_at) * CORES + core_at}

    core_dev = at(z, side, other_core)
    side_dev = at(z, other_side, core)

    def z_of(step):
        return lax.rem(z + step, zs)

    def send(src, dst, s_sem, r_sem, dev):
        return pltpu.make_async_remote_copy(
            src_ref=src, dst_ref=dst, send_sem=s_sem, recv_sem=r_sem, device_id=dev, device_id_type=pl.DeviceIdType.MESH
        )

    def up_copies(k):
        copies = []
        for block in range(fold):
            source = pl.ds(pl.multiple_of(block * width + k * CHUNK, CHUNK), CHUNK)
            target = pl.ds(block * CHUNK, CHUNK)
            for expert in range(EXP_G):
                copies.append(pltpu.make_async_copy(wg_ref.at[expert, source, :], wgb.at[k, expert, target, :], w_sem.at[k, 2 * (block * EXP_G + expert)]))
                copies.append(pltpu.make_async_copy(wu_ref.at[expert, source, :], wub.at[k, expert, target, :], w_sem.at[k, 2 * (block * EXP_G + expert) + 1]))
        return copies

    def down_copies(k):
        copies = []
        for block in range(fold):
            source = pl.ds(pl.multiple_of(block * width + k * CHUNK, CHUNK), CHUNK)
            for expert in range(EXP_G):
                copies.append(pltpu.make_async_copy(
                    wd_ref.at[expert, :, source],
                    wdb.at[k, pl.ds(expert * hidden, hidden), pl.ds(block * CHUNK, CHUNK)],
                    d_sem.at[k, block * EXP_G + expert],
                ))
        return copies

    def own_z(k, step):
        return send(x_ref.at[k], xb.at[k, core, side, z], az_s.at[k, step], az_r.at[k, step], at(z_of(step), side, core))

    def side_hop(k, step):
        spot = xb.at[k, core, side, z_of(step)]
        source = x_ref.at[k] if step == 0 else spot
        return send(source, spot, ay_s.at[k, step], ay_r.at[k, step], side_dev)

    def core_hop(k, half, half_index):
        return send(xb.at[k, core, half], xb.at[k, core, half], ac_s.at[k, half_index], ac_r.at[k, half_index], core_dev)

    def own_local(k):
        return pltpu.make_async_copy(x_ref.at[k], xb.at[k, core, side, z], own_sem.at[k])

    def route_z(step):
        return send(r_ref, rb.at[core, side, z], az_s.at[chunks, step], az_r.at[chunks, step], at(z_of(step), side, core))

    def route_side():
        return send(rb.at[core, side], rb.at[core, side], ay_s.at[chunks, 0], ay_r.at[chunks, 0], side_dev)

    def route_core():
        return send(rb.at[core], rb.at[core], ac_s.at[chunks, 0], ac_r.at[chunks, 0], core_dev)

    def route_local():
        return pltpu.make_async_copy(r_ref, rb.at[core, side, z], own_sem.at[chunks])

    for k in range(2):
        for copy in up_copies(k):
            copy.start()
    for k in range(chunks):
        own_local(k).start()
    route_local().start()

    barrier = pltpu.get_barrier_semaphore()
    for step in range(1, zs):
        pl.semaphore_signal(barrier, inc=1, device_id=at(z_of(step), side, core), device_id_type=pl.DeviceIdType.MESH)
    pl.semaphore_signal(barrier, inc=1, device_id=side_dev, device_id_type=pl.DeviceIdType.MESH)
    pl.semaphore_signal(barrier, inc=1, device_id=core_dev, device_id_type=pl.DeviceIdType.MESH)
    pl.semaphore_wait(barrier, zs + 1)

    @pl.loop(0, chunks)
    def _(k):
        side_hop(k, 0).start()
        for step in range(1, zs):
            own_z(k, step).start()

        @pl.when(k == 0)
        def _():
            for step in range(1, zs):
                route_z(step).start()

    @pl.loop(2, chunks)
    def _(k):
        for copy in up_copies(k):
            copy.start()

    @pl.loop(0, chunks)
    def _(k):
        for copy in down_copies(k):
            copy.start()

    size = fold * band
    def order(index):
        first = floor_div(index, band)
        rest = index - first * band
        second = floor_div(rest, rows)
        return second * band + first * rows + (rest - second * rows)

    perm[...] = (order(iota_f32((size, 1), 0)) == iota_f32((size, size), 1)).astype(F32).astype(BF16)
    perm_back[...] = (iota_f32((size, size), 0) == order(iota_f32((1, size), 1))).astype(F32).astype(BF16)
    acc[...] = jnp.zeros_like(acc)

    @pl.loop(0, chunks + 2)
    def _(now):
        @pl.when(now < chunks)
        def _():
            k = now
            for step in range(1, zs):
                back = zs - step
                send(x_ref.at[k], xb.at[k, core, side, z_of(back)], az_s.at[k, step], az_r.at[k, step], at(z_of(back), side, core)).wait_recv()
                side_hop(k, back).start()
            own_local(k).wait()
            core_hop(k, side, 0).start()

            @pl.when(k == 0)
            def _():
                route_local().wait()
                for step in range(1, zs):
                    route_z(step).wait_recv()
                route_side().start()

        @pl.when((now >= 1) & (now < chunks + 1))
        def _():
            k = now - 1
            for step in range(zs):
                spot = xb.at[k, core, other_side, z_of(step)]
                send(spot, spot, ay_s.at[k, step], ay_r.at[k, step], side_dev).wait_recv()
            core_hop(k, other_side, 1).start()

            @pl.when(k == 0)
            def _():
                send(rb.at[core, other_side], rb.at[core, other_side], ay_s.at[chunks, 0], ay_r.at[chunks, 0], side_dev).wait_recv()
                route_core().start()

        @pl.when(now >= 2)
        def _():
            k = now - 2
            for half_index, half in ((0, side), (1, other_side)):
                spot = xb.at[k, other_core, half]
                send(spot, spot, ac_s.at[k, half_index], ac_r.at[k, half_index], core_dev).wait_recv()
            for copy in up_copies(k):
                copy.wait()
            folded = xb[k].reshape(groups, size, CHUNK)
            straight = []
            for group in range(groups):
                moved = jnp.dot(perm[...], folded[group], preferred_element_type=F32).astype(BF16)
                straight.append(jnp.concatenate([moved[block * band:(block + 1) * band] for block in range(fold)], axis=1))
            left = jnp.concatenate(straight, axis=0)
            for expert in range(EXP_G):
                acc[2 * expert] += jnp.dot(left, wgb[k, expert], preferred_element_type=F32)
                acc[2 * expert + 1] += jnp.dot(left, wub[k, expert], preferred_element_type=F32)

    route_core_spot = rb.at[other_core]
    send(route_core_spot, route_core_spot, ac_s.at[chunks, 0], ac_r.at[chunks, 0], core_dev).wait_recv()
    total = units * rows
    line = iota_f32((1, units * pad_rows), 1)
    unit_of = floor_div(line, pad_rows)
    row_of = line - unit_of * pad_rows
    wanted = jnp.where(row_of < rows, unit_of * rows + row_of, -1.0)
    pick = (iota_f32((total, units * pad_rows), 0) == wanted).astype(F32).astype(BF16)
    scales = jnp.dot(pick, rb[...].reshape(units * pad_rows, LANES), preferred_element_type=F32)
    lane = lax.broadcasted_iota(jnp.int32, (total, LANES), 1)
    first_expert = me // (wide // GROUPS) * EXP_G
    for expert in range(EXP_G):
        scale = jnp.sum(jnp.where(lane == first_expert + expert, scales, 0.0), axis=1, keepdims=True)
        gate = acc[2 * expert]
        value = gate / (1.0 + jnp.exp(-gate)) * acc[2 * expert + 1]
        hid[:, expert * hidden:(expert + 1) * hidden] = (value * scale).astype(BF16)

    def back_core(k):
        return send(packed.at[k, other_core], got_core.at[k], bc_s.at[k], bc_r.at[k], core_dev)

    def back_side(k):
        return send(sum_side.at[k, other_side], got_side.at[k], by_s.at[k], by_r.at[k], side_dev)

    def back_z(k, step):
        return send(sum_z.at[k, z_of(step)], got_z.at[k, step], bz_s.at[k, step], bz_r.at[k, step], at(z_of(step), side, core))

    @pl.loop(0, chunks + 3)
    def _(now):
        @pl.when(now < chunks)
        def _():
            k = now
            for copy in down_copies(k):
                copy.wait()
            down = jnp.dot(hid[...], wdb[k], preferred_element_type=F32).astype(BF16)
            sets = []
            for group in range(groups):
                lines = down[group * band:(group + 1) * band]
                stacked = jnp.concatenate([lines[:, block * CHUNK:(block + 1) * CHUNK] for block in range(fold)], axis=0)
                sets.append(jnp.dot(perm_back[...], stacked, preferred_element_type=F32).astype(BF16))
            packed[k] = jnp.concatenate(sets, axis=0).reshape(CORES, SIDES, zs, unit, CHUNK)
            back_core(k).start()

        @pl.when((now >= 1) & (now < chunks + 1))
        def _():
            k = now - 1
            back_core(k).wait_recv()
            sum_side[k] = (packed[k, core].astype(F32) + got_core[k].astype(F32)).astype(BF16)
            back_side(k).start()

        @pl.when((now >= 2) & (now < chunks + 2))
        def _():
            k = now - 2
            back_side(k).wait_recv()
            sum_z[k] = (sum_side[k, side].astype(F32) + got_side[k].astype(F32)).astype(BF16)
            for step in range(1, zs):
                back_z(k, step).start()

        @pl.when(now >= 3)
        def _():
            k = now - 3
            done = sum_z[k, z].astype(F32)
            for step in range(1, zs):
                back_z(k, step).wait_recv()
                done = done + got_z[k, step].astype(F32)
            out_buf[k] = done.astype(BF16)
            pltpu.make_async_copy(out_buf.at[k], out_ref.at[k], out_sem.at[k]).start()

    @pl.loop(0, chunks)
    def _(k):
        for step in range(1, zs):
            own_z(k, step).wait_send()
            back_z(k, step).wait_send()
        for step in range(zs):
            side_hop(k, step).wait_send()
        core_hop(k, side, 0).wait_send()
        core_hop(k, other_side, 1).wait_send()
        back_core(k).wait_send()
        back_side(k).wait_send()
        pltpu.make_async_copy(out_buf.at[k], out_ref.at[k], out_sem.at[k]).wait()

    for step in range(1, zs):
        route_z(step).wait_send()
    route_side().wait_send()
    route_core().wait_send()


def local(wide, interpret, tokens, expert_ids, gates, w_gate, w_up, w_down):
    rows, model = tokens.shape
    hidden = w_gate.shape[2]
    fold = 16 // math.gcd(16, rows)
    width = model // fold
    chunks = width // CHUNK
    zs = wide // (CORES * SIDES)
    pad_rows = -(-rows // 16) * 16
    unit = rows * fold
    size = fold * unit
    total = wide * rows

    x = tokens.reshape(rows, fold, chunks, CHUNK).transpose(2, 1, 0, 3).reshape(chunks, unit, CHUNK)
    lanes = jnp.arange(LANES, dtype=jnp.int32)
    picked = expert_ids[:, :, None] == lanes[None, None, :]
    route = jnp.sum(jnp.where(picked, gates[:, :, None], 0.0), axis=1).astype(BF16)
    route = jnp.pad(route, ((0, pad_rows - rows), (0, 0)))

    any_space = pl.BlockSpec(memory_space=pl.ANY)
    dma = pltpu.SemaphoreType.DMA
    out = pl.pallas_call(
        functools.partial(kernel, wide, rows, fold),
        out_shape=jax.ShapeDtypeStruct((chunks, unit, CHUNK), BF16),
        in_specs=[any_space] * 5,
        out_specs=any_space,
        scratch_shapes=[
            pltpu.VMEM((chunks, CORES, SIDES, zs, unit, CHUNK), BF16),
            pltpu.VMEM((CORES, SIDES, zs, pad_rows, LANES), BF16),
            pltpu.VMEM((chunks, EXP_G, fold * CHUNK, hidden), BF16),
            pltpu.VMEM((chunks, EXP_G, fold * CHUNK, hidden), BF16),
            pltpu.VMEM((chunks, EXP_G * hidden, fold * CHUNK), BF16),
            pltpu.VMEM((2 * EXP_G, total, hidden), F32),
            pltpu.VMEM((total, EXP_G * hidden), BF16),
            pltpu.VMEM((size, size), BF16),
            pltpu.VMEM((size, size), BF16),
            pltpu.VMEM((chunks, CORES, SIDES, zs, unit, CHUNK), BF16),
            pltpu.VMEM((chunks, SIDES, zs, unit, CHUNK), BF16),
            pltpu.VMEM((chunks, SIDES, zs, unit, CHUNK), BF16),
            pltpu.VMEM((chunks, zs, unit, CHUNK), BF16),
            pltpu.VMEM((chunks, zs, unit, CHUNK), BF16),
            pltpu.VMEM((chunks, zs, unit, CHUNK), BF16),
            pltpu.VMEM((chunks, unit, CHUNK), BF16),
            dma((chunks, 2 * EXP_G * fold)),
            dma((chunks, EXP_G * fold)),
            dma((chunks + 1,)),
            dma((chunks + 1, zs)), dma((chunks + 1, zs)),
            dma((chunks + 1, zs)), dma((chunks + 1, zs)),
            dma((chunks + 1, 2)), dma((chunks + 1, 2)),
            dma((chunks, zs)), dma((chunks, zs)),
            dma((chunks,)), dma((chunks,)),
            dma((chunks,)), dma((chunks,)),
            dma((chunks,)),
        ],
        compiler_params=pltpu.CompilerParams(collective_id=0, has_side_effects=True, vmem_limit_bytes=67043328),
        **interpret,
    )(x, route, w_gate, w_up, w_down)
    return out.reshape(chunks, fold, rows, CHUNK).transpose(2, 1, 0, 3).reshape(rows, model)


def solution(mesh, interpret=None):
    return jax.shard_map(
        functools.partial(local, mesh.shape["wide"], interpret or {}),
        mesh=mesh,
        in_specs=(
            P(("parts", "wide"), None),
            P(("parts", "wide"), None),
            P(("parts", "wide"), None),
            P(None, None, "wide"),
            P(None, None, "wide"),
            P(None, "wide", None),
        ),
        out_specs=P(("parts", "wide"), None),
        check_vma=False,
    )
```

```python
import functools
import math

import jax
import jax.numpy as jnp
from jax import lax
from jax.experimental import pallas as pl
from jax.experimental.pallas import tpu as pltpu
from jax.sharding import PartitionSpec as P

GROUPS = 8
EXP_G = 2
CORES = 2
SIDES = 2
CHUNK = 256
LANES = 128
LAG_SIDE = 3
LAG_USE = 4
LAG_SUM = 1
LAG_Z = 4
LAG_END = 7
F32 = jnp.float32
BF16 = jnp.bfloat16


def floor_div(value, by):
    return jnp.floor((value + 0.5) * (1.0 / by))


def iota_f32(shape, dim):
    return lax.broadcasted_iota(jnp.int32, shape, dim).astype(F32)


def kernel(
    wide, rows, fold,
    tok_ref, ids_ref, gate_ref, wg_ref, wu_ref, wd_ref, out_ref,
    tok, x_ref, r_ref, xb, rb, wgb, wub, wdb, acc, hid, perm, perm_back, packed, got_core, sum_side, got_side, sum_z, got_z,
    tok_sem, w_sem, d_sem, own_sem, az_s, az_r, ay_s, ay_r, ac_s, ac_r, bz_s, bz_r, by_s, by_r, bc_s, bc_r,
):
    zs = wide // (CORES * SIDES)
    chunks = x_ref.shape[0]
    hidden = wg_ref.shape[2]
    width = chunks * CHUNK
    unit = rows * fold
    units = wide
    groups = units // fold
    band = fold * rows
    pad_rows = r_ref.shape[0]

    me = lax.axis_index("wide")
    core = lax.rem(me, CORES)
    chip = me // CORES
    side = lax.rem(chip, SIDES)
    z = chip // SIDES
    other_core = 1 - core
    other_side = 1 - side

    def at(z_at, side_at, core_at):
        return {"wide": (z_at * SIDES + side_at) * CORES + core_at}

    core_dev = at(z, side, other_core)
    side_dev = at(z, other_side, core)

    def z_of(step):
        return lax.rem(z + step, zs)

    def send(src, dst, s_sem, r_sem, dev):
        return pltpu.make_async_remote_copy(
            src_ref=src, dst_ref=dst, send_sem=s_sem, recv_sem=r_sem, device_id=dev, device_id_type=pl.DeviceIdType.MESH
        )

    def up_copies(k):
        copies = []
        for block in range(fold):
            source = pl.ds(pl.multiple_of(block * width + k * CHUNK, CHUNK), CHUNK)
            target = pl.ds(block * CHUNK, CHUNK)
            for expert in range(EXP_G):
                copies.append(pltpu.make_async_copy(wg_ref.at[expert, source, :], wgb.at[k, expert, target, :], w_sem.at[k, 2 * (block * EXP_G + expert)]))
                copies.append(pltpu.make_async_copy(wu_ref.at[expert, source, :], wub.at[k, expert, target, :], w_sem.at[k, 2 * (block * EXP_G + expert) + 1]))
        return copies

    def down_copies(k):
        copies = []
        for block in range(fold):
            source = pl.ds(pl.multiple_of(block * width + k * CHUNK, CHUNK), CHUNK)
            for expert in range(EXP_G):
                copies.append(pltpu.make_async_copy(
                    wd_ref.at[expert, :, source],
                    wdb.at[k, pl.ds(expert * hidden, hidden), pl.ds(block * CHUNK, CHUNK)],
                    d_sem.at[k, block * EXP_G + expert],
                ))
        return copies

    def own_z(k, step):
        return send(x_ref.at[k], xb.at[k, core, side, z], az_s.at[k, step], az_r.at[k, step], at(z_of(step), side, core))

    def side_hop(k, step):
        spot = xb.at[k, core, side, z_of(step)]
        source = x_ref.at[k] if step == 0 else spot
        return send(source, spot, ay_s.at[k, step], ay_r.at[k, step], side_dev)

    def core_hop(k, half, half_index):
        return send(xb.at[k, core, half], xb.at[k, core, half], ac_s.at[k, half_index], ac_r.at[k, half_index], core_dev)

    def own_local(k):
        return pltpu.make_async_copy(x_ref.at[k], xb.at[k, core, side, z], own_sem.at[k])

    def route_z(step):
        return send(r_ref, rb.at[core, side, z], az_s.at[chunks, step], az_r.at[chunks, step], at(z_of(step), side, core))

    def route_side():
        return send(rb.at[core, side], rb.at[core, side], ay_s.at[chunks, 0], ay_r.at[chunks, 0], side_dev)

    def route_core():
        return send(rb.at[core], rb.at[core], ac_s.at[chunks, 0], ac_r.at[chunks, 0], core_dev)

    def route_local():
        return pltpu.make_async_copy(r_ref, rb.at[core, side, z], own_sem.at[chunks])

    token_copy = pltpu.make_async_copy(tok_ref, tok, tok_sem)
    token_copy.start()
    for copy in up_copies(0):
        copy.start()

    barrier = pltpu.get_barrier_semaphore()
    for step in range(1, zs):
        pl.semaphore_signal(barrier, inc=1, device_id=at(z_of(step), side, core), device_id_type=pl.DeviceIdType.MESH)
    pl.semaphore_signal(barrier, inc=1, device_id=side_dev, device_id_type=pl.DeviceIdType.MESH)
    pl.semaphore_signal(barrier, inc=1, device_id=core_dev, device_id_type=pl.DeviceIdType.MESH)

    lane = lax.broadcasted_iota(jnp.int32, (rows, LANES), 1)
    route = jnp.zeros((rows, LANES), F32)
    for slot in range(ids_ref.shape[1]):
        route = route + jnp.where(ids_ref[:, slot:slot + 1] == lane, gate_ref[:, slot:slot + 1], 0.0)
    spread = (iota_f32((pad_rows, rows), 0) == iota_f32((pad_rows, rows), 1)).astype(F32).astype(BF16)
    r_ref[...] = jnp.dot(spread, route.astype(BF16), preferred_element_type=F32).astype(BF16)
    route_local().start()
    token_copy.wait()
    place = iota_f32((unit, rows), 0) - iota_f32((unit, rows), 1)
    into = [(place == block * rows).astype(F32).astype(BF16) for block in range(fold)]
    for k in range(chunks):
        parts = [jnp.dot(into[block], tok[:, block * width + k * CHUNK:block * width + (k + 1) * CHUNK], preferred_element_type=F32) for block in range(fold)]
        x_ref[k] = sum(parts[1:], parts[0]).astype(BF16)
        own_local(k).start()
        if k == 0:
            pl.semaphore_wait(barrier, zs + 1)
        side_hop(k, 0).start()
        for step in range(1, zs):
            own_z(k, step).start()
        if k == 0:
            for step in range(1, zs):
                route_z(step).start()
    @pl.loop(1, chunks)
    def _(k):
        for copy in up_copies(k):
            copy.start()

    @pl.loop(0, chunks)
    def _(k):
        for copy in down_copies(k):
            copy.start()

    size = fold * band
    def order(index):
        first = floor_div(index, band)
        rest = index - first * band
        second = floor_div(rest, rows)
        return second * band + first * rows + (rest - second * rows)

    perm[...] = (order(iota_f32((size, 1), 0)) == iota_f32((size, size), 1)).astype(F32).astype(BF16)
    perm_back[...] = (iota_f32((size, size), 0) == order(iota_f32((1, size), 1))).astype(F32).astype(BF16)
    acc[...] = jnp.zeros_like(acc)

    @pl.loop(0, chunks + LAG_USE)
    def _(now):
        @pl.when(now < chunks)
        def _():
            k = now
            for step in range(1, zs):
                back = zs - step
                send(x_ref.at[k], xb.at[k, core, side, z_of(back)], az_s.at[k, step], az_r.at[k, step], at(z_of(back), side, core)).wait_recv()
                side_hop(k, back).start()
            own_local(k).wait()
            core_hop(k, side, 0).start()

            @pl.when(k == 0)
            def _():
                route_local().wait()
                for step in range(1, zs):
                    route_z(step).wait_recv()
                route_side().start()

        @pl.when((now >= LAG_SIDE) & (now < chunks + LAG_SIDE))
        def _():
            k = now - LAG_SIDE
            for step in range(zs):
                spot = xb.at[k, core, other_side, z_of(step)]
                send(spot, spot, ay_s.at[k, step], ay_r.at[k, step], side_dev).wait_recv()
            core_hop(k, other_side, 1).start()

            @pl.when(k == 0)
            def _():
                send(rb.at[core, other_side], rb.at[core, other_side], ay_s.at[chunks, 0], ay_r.at[chunks, 0], side_dev).wait_recv()
                route_core().start()

        @pl.when(now >= LAG_USE)
        def _():
            k = now - LAG_USE
            for half_index, half in ((0, side), (1, other_side)):
                spot = xb.at[k, other_core, half]
                send(spot, spot, ac_s.at[k, half_index], ac_r.at[k, half_index], core_dev).wait_recv()
            for copy in up_copies(k):
                copy.wait()
            folded = xb[k].reshape(groups, size, CHUNK)
            straight = []
            for group in range(groups):
                moved = jnp.dot(perm[...], folded[group], preferred_element_type=F32).astype(BF16)
                straight.append(jnp.concatenate([moved[block * band:(block + 1) * band] for block in range(fold)], axis=1))
            left = jnp.concatenate(straight, axis=0)
            for expert in range(EXP_G):
                acc[2 * expert] += jnp.dot(left, wgb[k, expert], preferred_element_type=F32)
                acc[2 * expert + 1] += jnp.dot(left, wub[k, expert], preferred_element_type=F32)

    route_core_spot = rb.at[other_core]
    send(route_core_spot, route_core_spot, ac_s.at[chunks, 0], ac_r.at[chunks, 0], core_dev).wait_recv()
    total = units * rows
    line = iota_f32((1, units * pad_rows), 1)
    unit_of = floor_div(line, pad_rows)
    row_of = line - unit_of * pad_rows
    wanted = jnp.where(row_of < rows, unit_of * rows + row_of, -1.0)
    pick = (iota_f32((total, units * pad_rows), 0) == wanted).astype(F32).astype(BF16)
    scales = jnp.dot(pick, rb[...].reshape(units * pad_rows, LANES), preferred_element_type=F32)
    lane = lax.broadcasted_iota(jnp.int32, (total, LANES), 1)
    first_expert = me // (wide // GROUPS) * EXP_G
    for expert in range(EXP_G):
        scale = jnp.sum(jnp.where(lane == first_expert + expert, scales, 0.0), axis=1, keepdims=True)
        gate = acc[2 * expert]
        value = gate / (1.0 + jnp.exp(-gate)) * acc[2 * expert + 1]
        hid[:, expert * hidden:(expert + 1) * hidden] = (value * scale).astype(BF16)

    def back_core(k):
        return send(packed.at[k, other_core], got_core.at[k], bc_s.at[k], bc_r.at[k], core_dev)

    def back_side(k):
        return send(sum_side.at[k, other_side], got_side.at[k], by_s.at[k], by_r.at[k], side_dev)

    def back_z(k, step):
        return send(sum_z.at[k, z_of(step)], got_z.at[k, step], bz_s.at[k, step], bz_r.at[k, step], at(z_of(step), side, core))

    @pl.loop(0, chunks + LAG_END)
    def _(now):
        @pl.when(now < chunks)
        def _():
            k = now
            for copy in down_copies(k):
                copy.wait()
            down = jnp.dot(hid[...], wdb[k], preferred_element_type=F32).astype(BF16)
            sets = []
            for group in range(groups):
                lines = down[group * band:(group + 1) * band]
                stacked = jnp.concatenate([lines[:, block * CHUNK:(block + 1) * CHUNK] for block in range(fold)], axis=0)
                sets.append(jnp.dot(perm_back[...], stacked, preferred_element_type=F32).astype(BF16))
            packed[k] = jnp.concatenate(sets, axis=0).reshape(CORES, SIDES, zs, unit, CHUNK)
            back_core(k).start()

        @pl.when((now >= LAG_SUM) & (now < chunks + LAG_SUM))
        def _():
            k = now - LAG_SUM
            back_core(k).wait_recv()
            sum_side[k] = (packed[k, core].astype(F32) + got_core[k].astype(F32)).astype(BF16)
            back_side(k).start()

        @pl.when((now >= LAG_Z) & (now < chunks + LAG_Z))
        def _():
            k = now - LAG_Z
            back_side(k).wait_recv()
            sum_z[k] = (sum_side[k, side].astype(F32) + got_side[k].astype(F32)).astype(BF16)
            for step in range(1, zs):
                back_z(k, step).start()

        @pl.when(now >= LAG_END)
        def _():
            k = now - LAG_END
            done = sum_z[k, z].astype(F32)
            for step in range(1, zs):
                back_z(k, step).wait_recv()
                done = done + got_z[k, step].astype(F32)
            final = done.astype(BF16)
            away = iota_f32((rows, unit), 1) - iota_f32((rows, unit), 0)
            for block in range(fold):
                out_of = (away == block * rows).astype(F32).astype(BF16)
                spot = pl.ds(pl.multiple_of(block * width + k * CHUNK, CHUNK), CHUNK)
                out_ref[:, spot] = jnp.dot(out_of, final, preferred_element_type=F32).astype(BF16)

    @pl.loop(0, chunks)
    def _(k):
        for step in range(1, zs):
            own_z(k, step).wait_send()
            back_z(k, step).wait_send()
        for step in range(zs):
            side_hop(k, step).wait_send()
        core_hop(k, side, 0).wait_send()
        core_hop(k, other_side, 1).wait_send()
        back_core(k).wait_send()
        back_side(k).wait_send()

    for step in range(1, zs):
        route_z(step).wait_send()
    route_side().wait_send()
    route_core().wait_send()


def local(wide, interpret, tokens, expert_ids, gates, w_gate, w_up, w_down):
    rows, model = tokens.shape
    hidden = w_gate.shape[2]
    fold = 16 // math.gcd(16, rows)
    width = model // fold
    chunks = width // CHUNK
    zs = wide // (CORES * SIDES)
    pad_rows = -(-rows // 16) * 16
    unit = rows * fold
    size = fold * unit
    total = wide * rows

    any_space = pl.BlockSpec(memory_space=pl.ANY)
    dma = pltpu.SemaphoreType.DMA
    out = pl.pallas_call(
        functools.partial(kernel, wide, rows, fold),
        out_shape=jax.ShapeDtypeStruct((rows, model), BF16),
        in_specs=[any_space] + [pl.BlockSpec(memory_space=pltpu.VMEM)] * 2 + [any_space] * 3,
        out_specs=pl.BlockSpec(memory_space=pltpu.VMEM),
        scratch_shapes=[
            pltpu.VMEM((rows, model), BF16),
            pltpu.VMEM((chunks, unit, CHUNK), BF16),
            pltpu.VMEM((pad_rows, LANES), BF16),
            pltpu.VMEM((chunks, CORES, SIDES, zs, unit, CHUNK), BF16),
            pltpu.VMEM((CORES, SIDES, zs, pad_rows, LANES), BF16),
            pltpu.VMEM((chunks, EXP_G, fold * CHUNK, hidden), BF16),
            pltpu.VMEM((chunks, EXP_G, fold * CHUNK, hidden), BF16),
            pltpu.VMEM((chunks, EXP_G * hidden, fold * CHUNK), BF16),
            pltpu.VMEM((2 * EXP_G, total, hidden), F32),
            pltpu.VMEM((total, EXP_G * hidden), BF16),
            pltpu.VMEM((size, size), BF16),
            pltpu.VMEM((size, size), BF16),
            pltpu.VMEM((chunks, CORES, SIDES, zs, unit, CHUNK), BF16),
            pltpu.VMEM((chunks, SIDES, zs, unit, CHUNK), BF16),
            pltpu.VMEM((chunks, SIDES, zs, unit, CHUNK), BF16),
            pltpu.VMEM((chunks, zs, unit, CHUNK), BF16),
            pltpu.VMEM((chunks, zs, unit, CHUNK), BF16),
            pltpu.VMEM((chunks, zs, unit, CHUNK), BF16),
            dma(()),
            dma((chunks, 2 * EXP_G * fold)),
            dma((chunks, EXP_G * fold)),
            dma((chunks + 1,)),
            dma((chunks + 1, zs)), dma((chunks + 1, zs)),
            dma((chunks + 1, zs)), dma((chunks + 1, zs)),
            dma((chunks + 1, 2)), dma((chunks + 1, 2)),
            dma((chunks, zs)), dma((chunks, zs)),
            dma((chunks,)), dma((chunks,)),
            dma((chunks,)), dma((chunks,)),
        ],
        compiler_params=pltpu.CompilerParams(collective_id=0, has_side_effects=True, vmem_limit_bytes=67043328),
        **interpret,
    )(tokens, expert_ids, gates, w_gate, w_up, w_down)
    return out


def solution(mesh, interpret=None):
    return jax.shard_map(
        functools.partial(local, mesh.shape["wide"], interpret or {}),
        mesh=mesh,
        in_specs=(
            P(("parts", "wide"), None),
            P(("parts", "wide"), None),
            P(("parts", "wide"), None),
            P(None, None, "wide"),
            P(None, None, "wide"),
            P(None, "wide", None),
        ),
        out_specs=P(("parts", "wide"), None),
        check_vma=False,
    )
```

```python
import functools
import math

import jax
import jax.numpy as jnp
from jax import lax
from jax.experimental import pallas as pl
from jax.experimental.pallas import tpu as pltpu
from jax.sharding import PartitionSpec as P

GROUPS = 8
EXP_G = 2
CORES = 2
SIDES = 2
CHUNK = 256
LANES = 128
LAG_SIDE = 3
LAG_USE = 4
LAG_SUM = 1
LAG_Z = 4
LAG_END = 7
F32 = jnp.float32
BF16 = jnp.bfloat16


def floor_div(value, by):
    return jnp.floor((value + 0.5) * (1.0 / by))


def iota_f32(shape, dim):
    return lax.broadcasted_iota(jnp.int32, shape, dim).astype(F32)


def kernel(
    wide, rows, fold,
    tok_ref, ids_ref, gate_ref, wg_ref, wu_ref, wd_ref, out_ref,
    tok, x_ref, r_ref, xb, rb, wgb, wub, wdb, acc, hid, perm, perm_back, packed, got_core, sum_side, got_side, sum_z, got_z,
    tok_sem, w_sem, d_sem, own_sem, az_s, az_r, ay_s, ay_r, ac_s, ac_r, bz_s, bz_r, by_s, by_r, bc_s, bc_r,
):
    zs = wide // (CORES * SIDES)
    chunks = x_ref.shape[0]
    hidden = wg_ref.shape[2]
    width = chunks * CHUNK
    unit = rows * fold
    units = wide
    groups = units // fold
    band = fold * rows
    pad_rows = r_ref.shape[0]

    me = lax.axis_index("wide")
    core = lax.rem(me, CORES)
    chip = me // CORES
    side = lax.rem(chip, SIDES)
    z = chip // SIDES
    other_core = 1 - core
    other_side = 1 - side

    def at(z_at, side_at, core_at):
        return {"wide": (z_at * SIDES + side_at) * CORES + core_at}

    core_dev = at(z, side, other_core)
    side_dev = at(z, other_side, core)

    def z_of(step):
        return lax.rem(z + step, zs)

    def send(src, dst, s_sem, r_sem, dev):
        return pltpu.make_async_remote_copy(
            src_ref=src, dst_ref=dst, send_sem=s_sem, recv_sem=r_sem, device_id=dev, device_id_type=pl.DeviceIdType.MESH
        )

    def up_copies(k):
        copies = []
        for block in range(fold):
            source = pl.ds(pl.multiple_of(block * width + k * CHUNK, CHUNK), CHUNK)
            target = pl.ds(block * CHUNK, CHUNK)
            copies.append(pltpu.make_async_copy(wg_ref.at[:, source, :], wgb.at[k, :, target, :], w_sem.at[k, 2 * block]))
            copies.append(pltpu.make_async_copy(wu_ref.at[:, source, :], wub.at[k, :, target, :], w_sem.at[k, 2 * block + 1]))
        return copies

    def down_copies(k):
        copies = []
        for block in range(fold):
            source = pl.ds(pl.multiple_of(block * width + k * CHUNK, CHUNK), CHUNK)
            for expert in range(EXP_G):
                copies.append(pltpu.make_async_copy(
                    wd_ref.at[expert, :, source],
                    wdb.at[k, pl.ds(expert * hidden, hidden), pl.ds(block * CHUNK, CHUNK)],
                    d_sem.at[k, block * EXP_G + expert],
                ))
        return copies

    def own_z(k, step):
        return send(x_ref.at[k], xb.at[k, core, side, z], az_s.at[k, step], az_r.at[k, step], at(z_of(step), side, core))

    def side_hop(k, step):
        spot = xb.at[k, core, side, z_of(step)]
        source = x_ref.at[k] if step == 0 else spot
        return send(source, spot, ay_s.at[k, step], ay_r.at[k, step], side_dev)

    def core_hop(k, half, half_index):
        return send(xb.at[k, core, half], xb.at[k, core, half], ac_s.at[k, half_index], ac_r.at[k, half_index], core_dev)

    def own_local(k):
        return pltpu.make_async_copy(x_ref.at[k], xb.at[k, core, side, z], own_sem.at[k])

    def route_z(step):
        return send(r_ref, rb.at[core, side, z], az_s.at[chunks, step], az_r.at[chunks, step], at(z_of(step), side, core))

    def route_side():
        return send(rb.at[core, side], rb.at[core, side], ay_s.at[chunks, 0], ay_r.at[chunks, 0], side_dev)

    def route_core():
        return send(rb.at[core], rb.at[core], ac_s.at[chunks, 0], ac_r.at[chunks, 0], core_dev)

    def route_local():
        return pltpu.make_async_copy(r_ref, rb.at[core, side, z], own_sem.at[chunks])

    token_copy = pltpu.make_async_copy(tok_ref, tok, tok_sem)
    token_copy.start()
    for copy in up_copies(0):
        copy.start()

    barrier = pltpu.get_barrier_semaphore()
    for step in range(1, zs):
        pl.semaphore_signal(barrier, inc=1, device_id=at(z_of(step), side, core), device_id_type=pl.DeviceIdType.MESH)
    pl.semaphore_signal(barrier, inc=1, device_id=side_dev, device_id_type=pl.DeviceIdType.MESH)
    pl.semaphore_signal(barrier, inc=1, device_id=core_dev, device_id_type=pl.DeviceIdType.MESH)

    lane = lax.broadcasted_iota(jnp.int32, (rows, LANES), 1)
    route = jnp.zeros((rows, LANES), F32)
    for slot in range(ids_ref.shape[1]):
        route = route + jnp.where(ids_ref[:, slot:slot + 1] == lane, gate_ref[:, slot:slot + 1], 0.0)
    spread = (iota_f32((pad_rows, rows), 0) == iota_f32((pad_rows, rows), 1)).astype(F32).astype(BF16)
    r_ref[...] = jnp.dot(spread, route.astype(BF16), preferred_element_type=F32).astype(BF16)
    route_local().start()
    token_copy.wait()
    place = iota_f32((unit, rows), 0) - iota_f32((unit, rows), 1)
    into = [(place == block * rows).astype(F32).astype(BF16) for block in range(fold)]
    for k in range(chunks):
        parts = [jnp.dot(into[block], tok[:, block * width + k * CHUNK:block * width + (k + 1) * CHUNK], preferred_element_type=F32) for block in range(fold)]
        x_ref[k] = sum(parts[1:], parts[0]).astype(BF16)
        own_local(k).start()
        if k == 0:
            pl.semaphore_wait(barrier, zs + 1)
        side_hop(k, 0).start()
        for step in range(1, zs):
            own_z(k, step).start()
        if k == 0:
            for step in range(1, zs):
                route_z(step).start()
    size = fold * band
    def order(index):
        first = floor_div(index, band)
        rest = index - first * band
        second = floor_div(rest, rows)
        return second * band + first * rows + (rest - second * rows)

    perm[...] = (order(iota_f32((size, 1), 0)) == iota_f32((size, size), 1)).astype(F32).astype(BF16)
    perm_back[...] = (iota_f32((size, size), 0) == order(iota_f32((1, size), 1))).astype(F32).astype(BF16)
    acc[...] = jnp.zeros_like(acc)

    @pl.loop(0, chunks + LAG_USE)
    def _(now):
        @pl.when(now < chunks)
        def _():
            k = now
            for step in range(1, zs):
                back = zs - step
                send(x_ref.at[k], xb.at[k, core, side, z_of(back)], az_s.at[k, step], az_r.at[k, step], at(z_of(back), side, core)).wait_recv()
                side_hop(k, back).start()
            own_local(k).wait()
            core_hop(k, side, 0).start()

            @pl.when(k + 1 < chunks)
            def _():
                for copy in up_copies(k + 1):
                    copy.start()

            for copy in down_copies(k):
                copy.start()

            @pl.when(k == 0)
            def _():
                route_local().wait()
                for step in range(1, zs):
                    route_z(step).wait_recv()
                route_side().start()

        @pl.when((now >= LAG_SIDE) & (now < chunks + LAG_SIDE))
        def _():
            k = now - LAG_SIDE
            for step in range(zs):
                spot = xb.at[k, core, other_side, z_of(step)]
                send(spot, spot, ay_s.at[k, step], ay_r.at[k, step], side_dev).wait_recv()
            core_hop(k, other_side, 1).start()

            @pl.when(k == 0)
            def _():
                send(rb.at[core, other_side], rb.at[core, other_side], ay_s.at[chunks, 0], ay_r.at[chunks, 0], side_dev).wait_recv()
                route_core().start()

        @pl.when(now >= LAG_USE)
        def _():
            k = now - LAG_USE
            for half_index, half in ((0, side), (1, other_side)):
                spot = xb.at[k, other_core, half]
                send(spot, spot, ac_s.at[k, half_index], ac_r.at[k, half_index], core_dev).wait_recv()
            for copy in up_copies(k):
                copy.wait()
            folded = xb[k].reshape(groups, size, CHUNK)
            straight = []
            for group in range(groups):
                moved = jnp.dot(perm[...], folded[group], preferred_element_type=F32).astype(BF16)
                straight.append(jnp.concatenate([moved[block * band:(block + 1) * band] for block in range(fold)], axis=1))
            left = jnp.concatenate(straight, axis=0)
            for expert in range(EXP_G):
                acc[2 * expert] += jnp.dot(left, wgb[k, expert], preferred_element_type=F32)
                acc[2 * expert + 1] += jnp.dot(left, wub[k, expert], preferred_element_type=F32)

    route_core_spot = rb.at[other_core]
    send(route_core_spot, route_core_spot, ac_s.at[chunks, 0], ac_r.at[chunks, 0], core_dev).wait_recv()
    total = units * rows
    line = iota_f32((1, units * pad_rows), 1)
    unit_of = floor_div(line, pad_rows)
    row_of = line - unit_of * pad_rows
    wanted = jnp.where(row_of < rows, unit_of * rows + row_of, -1.0)
    pick = (iota_f32((total, units * pad_rows), 0) == wanted).astype(F32).astype(BF16)
    scales = jnp.dot(pick, rb[...].reshape(units * pad_rows, LANES), preferred_element_type=F32)
    lane = lax.broadcasted_iota(jnp.int32, (total, LANES), 1)
    first_expert = me // (wide // GROUPS) * EXP_G
    for expert in range(EXP_G):
        scale = jnp.sum(jnp.where(lane == first_expert + expert, scales, 0.0), axis=1, keepdims=True)
        gate = acc[2 * expert]
        value = gate / (1.0 + jnp.exp(-gate)) * acc[2 * expert + 1]
        hid[:, expert * hidden:(expert + 1) * hidden] = (value * scale).astype(BF16)

    def back_core(k):
        return send(packed.at[k, other_core], got_core.at[k], bc_s.at[k], bc_r.at[k], core_dev)

    def back_side(k):
        return send(sum_side.at[k, other_side], got_side.at[k], by_s.at[k], by_r.at[k], side_dev)

    def back_z(k, step):
        return send(sum_z.at[k, z_of(step)], got_z.at[k, step], bz_s.at[k, step], bz_r.at[k, step], at(z_of(step), side, core))

    @pl.loop(0, chunks + LAG_END)
    def _(now):
        @pl.when(now < chunks)
        def _():
            k = now
            for copy in down_copies(k):
                copy.wait()
            down = jnp.dot(hid[...], wdb[k], preferred_element_type=F32).astype(BF16)
            sets = []
            for group in range(groups):
                lines = down[group * band:(group + 1) * band]
                stacked = jnp.concatenate([lines[:, block * CHUNK:(block + 1) * CHUNK] for block in range(fold)], axis=0)
                sets.append(jnp.dot(perm_back[...], stacked, preferred_element_type=F32).astype(BF16))
            packed[k] = jnp.concatenate(sets, axis=0).reshape(CORES, SIDES, zs, unit, CHUNK)
            back_core(k).start()

        @pl.when((now >= LAG_SUM) & (now < chunks + LAG_SUM))
        def _():
            k = now - LAG_SUM
            back_core(k).wait_recv()
            sum_side[k] = (packed[k, core].astype(F32) + got_core[k].astype(F32)).astype(BF16)
            back_side(k).start()

        @pl.when((now >= LAG_Z) & (now < chunks + LAG_Z))
        def _():
            k = now - LAG_Z
            back_side(k).wait_recv()
            sum_z[k] = (sum_side[k, side].astype(F32) + got_side[k].astype(F32)).astype(BF16)
            for step in range(1, zs):
                back_z(k, step).start()

        @pl.when(now >= LAG_END)
        def _():
            k = now - LAG_END
            done = sum_z[k, z].astype(F32)
            for step in range(1, zs):
                back_z(k, step).wait_recv()
                done = done + got_z[k, step].astype(F32)
            final = done.astype(BF16)
            away = iota_f32((rows, unit), 1) - iota_f32((rows, unit), 0)
            for block in range(fold):
                out_of = (away == block * rows).astype(F32).astype(BF16)
                spot = pl.ds(pl.multiple_of(block * width + k * CHUNK, CHUNK), CHUNK)
                out_ref[:, spot] = jnp.dot(out_of, final, preferred_element_type=F32).astype(BF16)

    @pl.loop(0, chunks)
    def _(k):
        for step in range(1, zs):
            own_z(k, step).wait_send()
            back_z(k, step).wait_send()
        for step in range(zs):
            side_hop(k, step).wait_send()
        core_hop(k, side, 0).wait_send()
        core_hop(k, other_side, 1).wait_send()
        back_core(k).wait_send()
        back_side(k).wait_send()

    for step in range(1, zs):
        route_z(step).wait_send()
    route_side().wait_send()
    route_core().wait_send()


def local(wide, interpret, tokens, expert_ids, gates, w_gate, w_up, w_down):
    rows, model = tokens.shape
    hidden = w_gate.shape[2]
    fold = 16 // math.gcd(16, rows)
    width = model // fold
    chunks = width // CHUNK
    zs = wide // (CORES * SIDES)
    pad_rows = -(-rows // 16) * 16
    unit = rows * fold
    size = fold * unit
    total = wide * rows

    any_space = pl.BlockSpec(memory_space=pl.ANY)
    dma = pltpu.SemaphoreType.DMA
    out = pl.pallas_call(
        functools.partial(kernel, wide, rows, fold),
        out_shape=jax.ShapeDtypeStruct((rows, model), BF16),
        in_specs=[any_space] + [pl.BlockSpec(memory_space=pltpu.VMEM)] * 2 + [any_space] * 3,
        out_specs=pl.BlockSpec(memory_space=pltpu.VMEM),
        scratch_shapes=[
            pltpu.VMEM((rows, model), BF16),
            pltpu.VMEM((chunks, unit, CHUNK), BF16),
            pltpu.VMEM((pad_rows, LANES), BF16),
            pltpu.VMEM((chunks, CORES, SIDES, zs, unit, CHUNK), BF16),
            pltpu.VMEM((CORES, SIDES, zs, pad_rows, LANES), BF16),
            pltpu.VMEM((chunks, EXP_G, fold * CHUNK, hidden), BF16),
            pltpu.VMEM((chunks, EXP_G, fold * CHUNK, hidden), BF16),
            pltpu.VMEM((chunks, EXP_G * hidden, fold * CHUNK), BF16),
            pltpu.VMEM((2 * EXP_G, total, hidden), F32),
            pltpu.VMEM((total, EXP_G * hidden), BF16),
            pltpu.VMEM((size, size), BF16),
            pltpu.VMEM((size, size), BF16),
            pltpu.VMEM((chunks, CORES, SIDES, zs, unit, CHUNK), BF16),
            pltpu.VMEM((chunks, SIDES, zs, unit, CHUNK), BF16),
            pltpu.VMEM((chunks, SIDES, zs, unit, CHUNK), BF16),
            pltpu.VMEM((chunks, zs, unit, CHUNK), BF16),
            pltpu.VMEM((chunks, zs, unit, CHUNK), BF16),
            pltpu.VMEM((chunks, zs, unit, CHUNK), BF16),
            dma(()),
            dma((chunks, 2 * fold)),
            dma((chunks, EXP_G * fold)),
            dma((chunks + 1,)),
            dma((chunks + 1, zs)), dma((chunks + 1, zs)),
            dma((chunks + 1, zs)), dma((chunks + 1, zs)),
            dma((chunks + 1, 2)), dma((chunks + 1, 2)),
            dma((chunks, zs)), dma((chunks, zs)),
            dma((chunks,)), dma((chunks,)),
            dma((chunks,)), dma((chunks,)),
        ],
        compiler_params=pltpu.CompilerParams(collective_id=0, has_side_effects=True, vmem_limit_bytes=67043328),
        **interpret,
    )(tokens, expert_ids, gates, w_gate, w_up, w_down)
    return out


def solution(mesh, interpret=None):
    return jax.shard_map(
        functools.partial(local, mesh.shape["wide"], interpret or {}),
        mesh=mesh,
        in_specs=(
            P(("parts", "wide"), None),
            P(("parts", "wide"), None),
            P(("parts", "wide"), None),
            P(None, None, "wide"),
            P(None, None, "wide"),
            P(None, "wide", None),
        ),
        out_specs=P(("parts", "wide"), None),
        check_vma=False,
    )
```
